32 devices in a mesh: ops: 4 (over z), sec: 8 (over y, x, core).
Axes of the slice: x: 2, y: 2, z: 4, core: 2. Of those that a mesh axis runs over, the one named last changes fastest.
Arguments:
- wavefunction: float32 [512, 128, 128], P(('ops', 'sec')), may hold values from -6 to 6
- left_sector: int32 [512], P(('ops', 'sec')), may hold values from 0 to 15, as said below
- right_sector: int32 [512], P(('ops', 'sec')), may hold values from 0 to 1
- left_size: int32 [16], replicated, may hold values from 64 to 128
- right_size: int32 [2], replicated, may hold values from 64 to 128
- left_ops: float32 [16, 4, 128, 128], P('sec', 'ops'), may hold values from -0.25 to 0.25
- right_ops: float32 [2, 4, 128, 128], P(None, 'ops'), may hold values from -0.5 to 0.5
Outputs:
- sigma: float32 [512, 128, 128], P(('ops', 'sec'))
The draws below stay inside these ranges and needn't reach their ends.
Inputs may be any that keep to these rules, and one draw needn't show every extreme that they name: `left_sector`: the left sectors of the 16 blocks of one device are distinct and come in whole groups g * 2 to g * 2 + 1.
All inputs are finite; a program needn't handle non-finite values.
Results may differ from the reference program's by a relative error of at most 0.0003.
Values sent between devices are 32-bit elements; how exact they have to be, the bound alone decides.
A program may use at most 64 MiB of HBM per device.

```python
import jax
import jax.numpy as jnp
from jax import lax

W = 128
PAIR_DEV = 16
SEC_DEV = 2
RSECT = 2
TERMS = 4
LSECT = 16
BLOCKS = 512
N_OPS = 4
N_SEC = 8


def draw_left_sector(key, part):
    device_count = N_OPS * N_SEC
    group_count = PAIR_DEV // SEC_DEV
    popular = jax.random.randint(jax.random.fold_in(key, 11), (N_SEC,), 0, 1024)
    noise = jax.random.randint(jax.random.fold_in(key, 12), (device_count, N_SEC), 0, 1024)
    scores = (popular[None, :] + noise) * N_SEC + jnp.arange(N_SEC)[None, :]
    chosen = lax.top_k(scores, group_count)[1]
    sectors = chosen[:, :, None] * SEC_DEV + jnp.arange(SEC_DEV)[None, None, :]
    sectors = sectors.reshape(device_count, PAIR_DEV)
    shuffle = jax.random.randint(jax.random.fold_in(key, 13), (device_count, PAIR_DEV), 0, 65536) * PAIR_DEV + jnp.arange(PAIR_DEV)[None, :]
    order = jnp.argsort(shuffle, axis=1)
    return jnp.take_along_axis(sectors, order, axis=1).reshape(device_count * PAIR_DEV).astype(jnp.int32)


def place_ends(array, rng, low, largest):
    dims = array.shape
    place = [jax.random.randint(jax.random.fold_in(rng, axis), (), 0, dims[axis]) for axis in range(len(dims))]
    array = array.at[tuple(place)].set(low)
    longest = dims.index(max(dims))
    place[longest] = (place[longest] + 1) % dims[longest]
    return array.at[tuple(place)].set(largest)


def level_of(rng, extent, split, least, top_value):
    gain, own = 1.0, jax.random.fold_in(rng, 6)
    for dim, blocks in split:
        draws = jnp.exp(jax.random.uniform(jax.random.fold_in(own, dim), (blocks,), jnp.float32, least / len(split), top_value / len(split)))
        gain = gain * jnp.repeat(draws, extent[dim] // blocks).reshape([-1 if axis == dim else 1 for axis in range(len(extent))])
    return gain


def gaussian(own_key, shape, spread, reach, shards=(), kind=jnp.bfloat16):
    entries = jax.random.normal(own_key, shape, jnp.float32) * spread
    if len(shards) > 0:
        entries = level_of(own_key, shape, shards, -0.22, 0.18) * entries
    return jnp.clip(entries, min=-reach, max=reach).astype(kind)


def setup_inputs(seed: int = 0) -> dict:
    key_list = jax.random.split(jax.random.key(seed), 8)
    return {
        "wavefunction": gaussian(key_list[0], (BLOCKS, W, W), 1.0, 6.0, ((0, 32),), jnp.float32),
        "left_sector": draw_left_sector(jax.random.fold_in(key_list[7], 71), 0),
        "right_sector": place_ends(jax.random.randint(key_list[2], (BLOCKS,), 0, RSECT), jax.random.fold_in(key_list[2], 1), 0, RSECT - 1).astype(jnp.int32),
        "left_size": place_ends(jax.random.randint(key_list[3], (LSECT,), W // 2, W + 1), jax.random.fold_in(key_list[3], 1), W // 2, W).astype(jnp.int32),
        "right_size": jax.random.randint(key_list[4], (RSECT,), W // 2, W + 1).astype(jnp.int32),
        "left_ops": gaussian(key_list[5], (LSECT, TERMS, W, W), (W * TERMS) ** -0.5, 0.25, ((0, 8), (1, 4)), jnp.float32),
        "right_ops": gaussian(key_list[6], (RSECT, TERMS, W, W), W ** -0.5, 0.5, ((1, 4),), jnp.float32),
    }


def reference(wavefunction, left_sector, right_sector, left_size, right_size, left_ops, right_ops):
    position = jnp.arange(W)

    def single(inputs):
        block, left_id, right_id = inputs
        row_live = position < left_size[left_id]
        col_live = position < right_size[right_id]
        window = (row_live[:, None] & col_live[None, :]).astype(jnp.float32)
        masked = block * window
        left_pick = left_ops[left_id]
        right_pick = right_ops[right_id]
        halfway = jnp.einsum('ij,tlj->til', masked, right_pick, precision=lax.Precision.HIGHEST)
        result = jnp.einsum('tmi,til->ml', left_pick, halfway, precision=lax.Precision.HIGHEST)
        return result * window

    return lax.map(single, (wavefunction, left_sector, right_sector))
```

```python
import jax
import jax.numpy as jnp
from jax import lax
from jax.experimental import pallas as pl
from jax.experimental.pallas import tpu as pltpu
from jax.sharding import PartitionSpec as P

MESH = pl.DeviceIdType.MESH


def contract(running, packed, left_ids, right_ids, live_count, left_blocks, right_blocks):
    turn_count = (live_count + 1) // 2

    def advance(turn_index, current):
        first = 2 * turn_index
        block = lax.dynamic_slice_in_dim(packed, first, 2, 0)
        left_sel = lax.dynamic_slice_in_dim(left_ids, first, 2, 0)
        right_sel = lax.dynamic_slice_in_dim(right_ids, first, 2, 0)
        left_pick = left_blocks[left_sel]
        right_pick = right_blocks[right_sel]
        halfway = jnp.einsum("sij,stlj->stil", block, right_pick, precision=lax.Precision.HIGHEST)
        update = jnp.einsum("stmi,stil->sml", left_pick, halfway, precision=lax.Precision.HIGHEST)
        before = lax.dynamic_slice_in_dim(current, first, 2, 0)
        return lax.dynamic_update_slice_in_dim(current, before + update, first, 0)

    return lax.fori_loop(0, turn_count, advance, running)


def gather_whole(left_ops, right_ops):
    return (
        lax.all_gather(left_ops, "ops", axis=1, tiled=True),
        lax.all_gather(right_ops, "ops", axis=1, tiled=True),
    )


def arrange(incoming, tags, slot_count, width):
    incoming = incoming.reshape(slot_count, width, width)
    tag_ids = tags.reshape(slot_count).astype(jnp.int32)
    live_flag = (tag_ids > 0).astype(jnp.int32)
    order = jnp.argsort(1 - live_flag, stable=True)
    live_count = jnp.sum(live_flag)
    packed = incoming[order]
    right_ids = jnp.maximum(tag_ids[order] - 1, 0)
    return (packed, right_ids, order, live_count)


def shards(wavefunction, left_sector, right_sector, left_size, right_size, left_ops, right_ops):
    peer_count = lax.axis_size("sec")
    sec_local = left_ops.shape[0]
    width = wavefunction.shape[1]
    position = jnp.arange(width)
    left_live = jnp.sum(
        jnp.where(
            left_sector[:, None] == jnp.arange(left_size.shape[0])[None, :], left_size[None, :], 0
        ),
        axis=1,
    )
    right_live = jnp.sum(
        jnp.where(
            right_sector[:, None] == jnp.arange(right_size.shape[0])[None, :],
            right_size[None, :],
            0,
        ),
        axis=1,
    )
    row_live = position[None, :] < left_live[:, None]
    col_live = position[None, :] < right_live[:, None]
    window = (row_live[:, :, None] & col_live[:, None, :]).astype(jnp.float32)
    masked = wavefunction * window
    owner = left_sector // sec_local
    within = left_sector % sec_local
    outgoing = (
        jnp.zeros((peer_count, sec_local, width, width), jnp.float32).at[owner, within].set(masked)
    )
    labels = (
        jnp.zeros((peer_count, sec_local), jnp.float32)
        .at[owner, within]
        .set((right_sector + 1).astype(jnp.float32))
    )
    incoming, tags = (
        lax.all_to_all(outgoing, "sec", split_axis=0, concat_axis=0, tiled=True),
        lax.all_to_all(labels, "sec", split_axis=0, concat_axis=0, tiled=True),
    )
    slot_count = peer_count * sec_local
    packed, right_ids, order, live_count = arrange(incoming, tags, slot_count, width)
    left_ids = order % sec_local
    empty = jnp.zeros_like(packed)
    left_all, right_all = gather_whole(left_ops, right_ops)
    result = contract(empty, packed, left_ids, right_ids, live_count, left_all, right_all)
    restored = jnp.zeros_like(result).at[order].set(result)
    returned = lax.all_to_all(
        restored.reshape(peer_count, sec_local, width, width),
        "sec",
        split_axis=0,
        concat_axis=0,
        tiled=True,
    )
    return returned[owner, within] * window


def term_orders(count):
    orders = []
    for here in range(count):
        orders.append(sorted(range(count), key=lambda t: (abs(t - here), abs(2 * t - count + 1), t)))
    return orders


def split(value):
    high = value.astype(jnp.bfloat16)
    low = (value - high.astype(jnp.float32)).astype(jnp.bfloat16)
    return high, low


def gather_contract(
    wf_hbm, lops_hbm, rops_hbm, lsec, rsec, lsize, rsize,
    out_ref,
    wbuf, lbuf, rbuf, mcat, hcat, acc, inverse, right_of,
    own_sem, recv_l, recv_r, send_x, send_y, send_up, send_dn, send_sib,
):
    terms = lax.axis_size("ops")
    sectors, _, width, _ = lbuf.shape
    rights = rbuf.shape[1]
    half = width // 2
    z = lax.axis_index("ops")
    sec = lax.axis_index("sec")
    core = sec % 2
    xpos = (sec // 2) % 2
    ypos = sec // 4
    sib = sec + 1 - 2 * core
    xnb = sec + 2 - 4 * xpos
    ynb = sec + 4 - 8 * ypos
    dnb = xnb + 4 - 8 * ypos
    has_up = z < terms - 1
    has_dn = z > 0
    table = term_orders(terms)
    order = []
    for k in range(terms):
        value = table[0][k] * 1
        for here in range(1, terms):
            value = jnp.where(z == here, table[here][k], value)
        order.append(value)

    def flip(group):
        return group + 1 - 2 * core

    barrier = pltpu.get_barrier_semaphore()

    def greet(zz, ss):
        pl.semaphore_signal(barrier, inc=1, device_id=(zz, ss), device_id_type=MESH)

    for peer in (sib, xnb, ynb):
        greet(z, peer)

    @pl.when(has_up)
    def _():
        greet(z + 1, sec)

    @pl.when(has_dn)
    def _():
        greet(z - 1, sec)

    own_l = [
        pltpu.make_async_copy(lops_hbm.at[i, 0], lbuf.at[2 * sec + i, z], recv_l.at[2 * sec + i, z])
        for i in range(2)
    ]
    own_r = pltpu.make_async_copy(rops_hbm.at[:, 0], rbuf.at[z], own_sem.at[0])
    own_w = pltpu.make_async_copy(wf_hbm, wbuf, own_sem.at[1])
    own_w.start()
    own_r.start()
    for copy in own_l:
        copy.start()
    pl.semaphore_wait(barrier, 3 + has_up.astype(jnp.int32) + has_dn.astype(jnp.int32))

    def move(src, dst, ssem, rsem, zz, ss):
        return pltpu.make_async_remote_copy(
            src_ref=src, dst_ref=dst, send_sem=ssem, recv_sem=rsem,
            device_id=(zz, ss), device_id_type=MESH,
        )

    def piece(group, i, t, ssem, zz, ss, own=False):
        s = 2 * group + i
        src = lops_hbm.at[i, 0] if own else lbuf.at[s, t]
        return move(src, lbuf.at[s, t], ssem, recv_l.at[s, t], zz, ss)

    def rpiece(h, t, ssem, zz, ss, own=False):
        rows = pl.ds(pl.multiple_of(h * half, half), half)
        src = rops_hbm.at[:, 0, rows] if own else rbuf.at[t, :, rows]
        return move(src, rbuf.at[t, :, rows], ssem, recv_r.at[t, h], zz, ss)

    def await_l(group, i, t):
        piece(group, i, t, send_x.at[t, 0], z, xnb).wait_recv()

    def await_r(h, t):
        rpiece(h, t, send_x.at[t, 0], z, xnb).wait_recv()

    def along(make, j, t, own, act):
        up = has_up & (t <= z)
        dn = has_dn & (t >= z)

        @pl.when(up)
        def _():
            act(make(t, send_up.at[t, j], z + 1, sec, own))

        @pl.when(dn)
        def _():
            act(make(t, send_dn.at[t, j], z - 1, sec, own))

    def fan_own(i, t, own, act):
        along(lambda t, ssem, zz, ss, own: piece(sec, i, t, ssem, zz, ss, own), i, t, own, act)
        act(piece(sec, i, t, send_x.at[t, i], z, xnb, own))
        act(piece(sec, i, t, send_y.at[t, i], z, ynb, own))
        act(piece(sec, i, t, send_sib.at[t, i], z, sib, own))

    def fan_right(t, own, act):
        along(lambda t, ssem, zz, ss, own: rpiece(core, t, ssem, zz, ss, own), 2, t, own, act)
        if not own:
            act(rpiece(core, t, send_sib.at[t, 8], z, sib))

    def fan_x(i, t, act):
        if i == 0:
            act(piece(xnb, i, t, send_y.at[t, 2], z, ynb))
        act(piece(xnb, i, t, send_sib.at[t, 2 + i], z, sib))

    def fan_y(i, t, act):
        if i == 1:
            act(piece(ynb, i, t, send_x.at[t, 2], z, xnb))
        act(piece(ynb, i, t, send_sib.at[t, 4 + i], z, sib))

    def fan_d(i, t, act):
        act(piece(dnb, i, t, send_sib.at[t, 6 + i], z, sib))

    start = lambda copy: copy.start()
    drain = lambda copy: copy.wait_send()

    t0 = order[0]
    for i in range(2):
        fan_own(i, t0, True, start)
    fan_right(t0, True, start)

    for s in range(sectors):
        value = jnp.int32(0)
        for p in range(1, sectors):
            value = jnp.where(lsec[p] == s, p, value)
        inverse[s] = value
        right_of[s] = rsec[value]

    row_at = lax.broadcasted_iota(jnp.int32, (width, width), 0)
    col_at = lax.broadcasted_iota(jnp.int32, (width, width), 1)

    own_w.wait()

    @pl.loop(0, sectors)
    def _(s):
        live = (row_at < lsize[s]) & (col_at < rsize[right_of[s]])
        high, low = split(jnp.where(live, wbuf[inverse[s]], 0.0))
        rows = pl.ds(pl.multiple_of(s * width, width), width)
        mcat[rows, :width] = high
        mcat[rows, width:] = low
        acc[s] = jnp.zeros((width, width), jnp.float32)

    own_r.wait()
    batch = 4 if sectors % 4 == 0 else 1

    def halfway(t):
        high, low = split(rbuf[t].reshape(rights * width, width))
        doubled = jnp.concatenate([high, high], axis=1)
        contract_last = (((1,), (1,)), ((), ()))

        @pl.loop(0, sectors // batch)
        def _(n):
            rows = pl.ds(pl.multiple_of(n * batch * width, batch * width), batch * width)
            left = mcat[rows, :]
            both = lax.dot_general(left, doubled, contract_last, preferred_element_type=jnp.float32)
            both += lax.dot_general(
                left[:, :width], low, contract_last, preferred_element_type=jnp.float32
            )
            for j in range(batch):
                s = n * batch + j
                mine = both[j * width : (j + 1) * width]
                which = jnp.full((width, width), right_of[s], jnp.int32)
                pick = mine[:, :width]
                for b in range(1, rights):
                    pick = jnp.where(which == b, mine[:, b * width : (b + 1) * width], pick)
                h_high, h_low = split(pick)
                hcat[t, s, :, :width] = h_high
                hcat[t, s, :, width:] = h_low

    def apply_left(s, t):
        high, low = split(lbuf[s, t])
        wide = jnp.dot(
            jnp.concatenate([high, low], axis=0), hcat[t, s], preferred_element_type=jnp.float32
        )
        acc[s] += wide[:width, :width] + (wide[:width, width:] + wide[width:, :width])

    def apply_group(group, t, wait):
        if wait:
            for i in range(2):
                await_l(group, i, t)
        for i in range(2):
            apply_left(2 * group + i, t)

    for k in range(terms + 2):
        if 1 <= k < terms:
            for i in range(2):
                await_l(sec, i, order[k])
                fan_own(i, order[k], False, start)
        if 1 <= k <= terms:
            t = order[k - 1]
            for i in range(2):
                await_l(xnb, i, t)
                fan_x(i, t, start)
                await_l(ynb, i, t)
                fan_y(i, t, start)
        if 2 <= k:
            t = order[k - 2]
            for i in range(2):
                await_l(dnb, i, t)
                fan_d(i, t, start)
        if 1 <= k < terms:
            await_r(core, order[k])
            fan_right(order[k], False, start)
        if 1 <= k <= terms:
            t = order[k - 1]
            apply_group(xnb, t, False)
            apply_group(ynb, t, False)
            apply_group(flip(xnb), t, True)
            apply_group(flip(ynb), t, True)
        if 2 <= k:
            t = order[k - 2]
            apply_group(dnb, t, False)
            apply_group(flip(dnb), t, True)
        if k < terms:
            t = order[k]
            if k >= 1:
                await_r(1 - core, t)
            else:
                for copy in own_l:
                    copy.wait()
            halfway(t)
            apply_group(sec, t, False)
            apply_group(sib, t, True)

    @pl.loop(0, sectors)
    def _(p):
        s = lsec[p]
        live = (row_at < lsize[s]) & (col_at < rsize[rsec[p]])
        out_ref[p] = jnp.where(live, acc[s], 0.0)

    for k in range(terms):
        t = order[k]
        for i in range(2):
            fan_own(i, t, k == 0, drain)
            fan_x(i, t, drain)
            fan_y(i, t, drain)
            fan_d(i, t, drain)
        fan_right(t, k == 0, drain)


def local_shards(wavefunction, left_sector, right_sector, left_size, right_size, left_ops, right_ops):
    terms = lax.axis_size("ops")
    sectors, width = left_size.shape[0], wavefunction.shape[1]
    rights = right_size.shape[0]
    dma = pltpu.SemaphoreType.DMA
    anywhere = pl.BlockSpec(memory_space=pl.ANY)
    scalars = pl.BlockSpec(memory_space=pltpu.SMEM)
    return pl.pallas_call(
        gather_contract,
        out_shape=jax.ShapeDtypeStruct(wavefunction.shape, jnp.float32),
        in_specs=[anywhere] * 3 + [scalars] * 4,
        out_specs=pl.BlockSpec(memory_space=pltpu.VMEM),
        scratch_shapes=[
            pltpu.VMEM((sectors, width, width), jnp.float32),
            pltpu.VMEM((sectors, terms, width, width), jnp.float32),
            pltpu.VMEM((terms, rights, width, width), jnp.float32),
            pltpu.VMEM((sectors * width, 2 * width), jnp.bfloat16),
            pltpu.VMEM((terms, sectors, width, 2 * width), jnp.bfloat16),
            pltpu.VMEM((sectors, width, width), jnp.float32),
            pltpu.SMEM((sectors,), jnp.int32),
            pltpu.SMEM((sectors,), jnp.int32),
            dma((2,)),
            dma((sectors, terms)),
            dma((terms, 2)),
            dma((terms, 3)),
            dma((terms, 3)),
            dma((terms, 3)),
            dma((terms, 3)),
            dma((terms, 9)),
        ],
        compiler_params=pltpu.CompilerParams(collective_id=0, has_side_effects=True),
    )(wavefunction, left_ops, right_ops, left_sector, right_sector, left_size, right_size)


def cube_shards(*arrays):
    wavefunction, left_size, left_ops = arrays[0], arrays[3], arrays[5]
    sectors, width = left_size.shape[0], wavefunction.shape[1]
    terms = lax.axis_size("ops")
    every_sector = wavefunction.shape[0] == sectors
    cube = lax.axis_size("sec") == 2**3 and left_ops.shape[:2] == (2, 1)
    small = sectors * terms * width * width * 4 <= 2**23
    if every_sector and cube and small:
        return local_shards(*arrays)
    return shards(*arrays)


def solution(mesh):
    placed = (
        P(("ops", "sec"), None, None),
        P(("ops", "sec")),
        P(("ops", "sec")),
        P(),
        P(),
        P("sec", "ops", None, None),
        P(None, "ops", None, None),
    )
    return jax.shard_map(
        cube_shards, mesh=mesh, in_specs=placed, out_specs=P(("ops", "sec"), None, None), check_vma=False
    )
```

```python
import jax
import jax.numpy as jnp
from jax import lax
from jax.experimental import pallas as pl
from jax.experimental.pallas import tpu as pltpu
from jax.sharding import PartitionSpec as P

MESH = pl.DeviceIdType.MESH


def contract(running, packed, left_ids, right_ids, live_count, left_blocks, right_blocks):
    turn_count = (live_count + 1) // 2

    def advance(turn_index, current):
        first = 2 * turn_index
        block = lax.dynamic_slice_in_dim(packed, first, 2, 0)
        left_sel = lax.dynamic_slice_in_dim(left_ids, first, 2, 0)
        right_sel = lax.dynamic_slice_in_dim(right_ids, first, 2, 0)
        left_pick = left_blocks[left_sel]
        right_pick = right_blocks[right_sel]
        halfway = jnp.einsum("sij,stlj->stil", block, right_pick, precision=lax.Precision.HIGHEST)
        update = jnp.einsum("stmi,stil->sml", left_pick, halfway, precision=lax.Precision.HIGHEST)
        before = lax.dynamic_slice_in_dim(current, first, 2, 0)
        return lax.dynamic_update_slice_in_dim(current, before + update, first, 0)

    return lax.fori_loop(0, turn_count, advance, running)


def gather_whole(left_ops, right_ops):
    return (
        lax.all_gather(left_ops, "ops", axis=1, tiled=True),
        lax.all_gather(right_ops, "ops", axis=1, tiled=True),
    )


def arrange(incoming, tags, slot_count, width):
    incoming = incoming.reshape(slot_count, width, width)
    tag_ids = tags.reshape(slot_count).astype(jnp.int32)
    live_flag = (tag_ids > 0).astype(jnp.int32)
    order = jnp.argsort(1 - live_flag, stable=True)
    live_count = jnp.sum(live_flag)
    packed = incoming[order]
    right_ids = jnp.maximum(tag_ids[order] - 1, 0)
    return (packed, right_ids, order, live_count)


def shards(wavefunction, left_sector, right_sector, left_size, right_size, left_ops, right_ops):
    peer_count = lax.axis_size("sec")
    sec_local = left_ops.shape[0]
    width = wavefunction.shape[1]
    position = jnp.arange(width)
    left_live = jnp.sum(
        jnp.where(
            left_sector[:, None] == jnp.arange(left_size.shape[0])[None, :], left_size[None, :], 0
        ),
        axis=1,
    )
    right_live = jnp.sum(
        jnp.where(
            right_sector[:, None] == jnp.arange(right_size.shape[0])[None, :],
            right_size[None, :],
            0,
        ),
        axis=1,
    )
    row_live = position[None, :] < left_live[:, None]
    col_live = position[None, :] < right_live[:, None]
    window = (row_live[:, :, None] & col_live[:, None, :]).astype(jnp.float32)
    masked = wavefunction * window
    owner = left_sector // sec_local
    within = left_sector % sec_local
    outgoing = (
        jnp.zeros((peer_count, sec_local, width, width), jnp.float32).at[owner, within].set(masked)
    )
    labels = (
        jnp.zeros((peer_count, sec_local), jnp.float32)
        .at[owner, within]
        .set((right_sector + 1).astype(jnp.float32))
    )
    incoming, tags = (
        lax.all_to_all(outgoing, "sec", split_axis=0, concat_axis=0, tiled=True),
        lax.all_to_all(labels, "sec", split_axis=0, concat_axis=0, tiled=True),
    )
    slot_count = peer_count * sec_local
    packed, right_ids, order, live_count = arrange(incoming, tags, slot_count, width)
    left_ids = order % sec_local
    empty = jnp.zeros_like(packed)
    left_all, right_all = gather_whole(left_ops, right_ops)
    result = contract(empty, packed, left_ids, right_ids, live_count, left_all, right_all)
    restored = jnp.zeros_like(result).at[order].set(result)
    returned = lax.all_to_all(
        restored.reshape(peer_count, sec_local, width, width),
        "sec",
        split_axis=0,
        concat_axis=0,
        tiled=True,
    )
    return returned[owner, within] * window


def term_orders(count):
    orders = []
    for here in range(count):
        orders.append(sorted(range(count), key=lambda t: (abs(t - here), abs(2 * t - count + 1), t)))
    return orders


def split(value):
    high = value.astype(jnp.bfloat16)
    low = (value - high.astype(jnp.float32)).astype(jnp.bfloat16)
    return high, low


def gather_contract(
    wf_hbm, lops_hbm, rops_hbm, lsec, rsec, lsize, rsize,
    out_ref,
    wbuf, lbuf, rbuf, mcat, hcat, acc, inverse, right_of,
    own_sem, recv_l, recv_r, send_x, send_y, send_up, send_dn, send_sib,
):
    terms = lax.axis_size("ops")
    sectors, _, width, _ = lbuf.shape
    rights = rbuf.shape[1]
    half = width // 2
    z = lax.axis_index("ops")
    sec = lax.axis_index("sec")
    core = sec % 2
    xpos = (sec // 2) % 2
    ypos = sec // 4
    sib = sec + 1 - 2 * core
    xnb = sec + 2 - 4 * xpos
    ynb = sec + 4 - 8 * ypos
    dnb = xnb + 4 - 8 * ypos
    has_up = z < terms - 1
    has_dn = z > 0
    table = term_orders(terms)
    order = []
    for k in range(terms):
        value = table[0][k] * 1
        for here in range(1, terms):
            value = jnp.where(z == here, table[here][k], value)
        order.append(value)

    def flip(group):
        return group + 1 - 2 * core

    barrier = pltpu.get_barrier_semaphore()

    def greet(zz, ss):
        pl.semaphore_signal(barrier, inc=1, device_id=(zz, ss), device_id_type=MESH)

    for peer in (sib, xnb, ynb):
        greet(z, peer)

    @pl.when(has_up)
    def _():
        greet(z + 1, sec)

    @pl.when(has_dn)
    def _():
        greet(z - 1, sec)

    own_l = [
        pltpu.make_async_copy(lops_hbm.at[i, 0], lbuf.at[2 * sec + i, z], recv_l.at[2 * sec + i, z])
        for i in range(2)
    ]
    own_r = pltpu.make_async_copy(rops_hbm.at[:, 0], rbuf.at[z], own_sem.at[0])
    own_w = pltpu.make_async_copy(wf_hbm, wbuf, own_sem.at[1])
    own_w.start()
    own_r.start()
    for copy in own_l:
        copy.start()
    pl.semaphore_wait(barrier, 3 + has_up.astype(jnp.int32) + has_dn.astype(jnp.int32))

    def move(src, dst, ssem, rsem, zz, ss):
        return pltpu.make_async_remote_copy(
            src_ref=src, dst_ref=dst, send_sem=ssem, recv_sem=rsem,
            device_id=(zz, ss), device_id_type=MESH,
        )

    def piece(group, i, t, ssem, zz, ss, own=False):
        s = 2 * group + i
        src = lops_hbm.at[i, 0] if own else lbuf.at[s, t]
        return move(src, lbuf.at[s, t], ssem, recv_l.at[s, t], zz, ss)

    def rpiece(h, t, ssem, zz, ss, own=False):
        rows = pl.ds(pl.multiple_of(h * half, half), half)
        src = rops_hbm.at[:, 0, rows] if own else rbuf.at[t, :, rows]
        return move(src, rbuf.at[t, :, rows], ssem, recv_r.at[t, h], zz, ss)

    def await_l(group, i, t):
        piece(group, i, t, send_x.at[t, 0], z, xnb).wait_recv()

    def await_r(h, t):
        rpiece(h, t, send_x.at[t, 0], z, xnb).wait_recv()

    def along(make, j, t, own, act):
        up = has_up & (t <= z)
        dn = has_dn & (t >= z)

        @pl.when(up)
        def _():
            act(make(t, send_up.at[t, j], z + 1, sec, own))

        @pl.when(dn)
        def _():
            act(make(t, send_dn.at[t, j], z - 1, sec, own))

    def fan_own(i, t, own, act):
        along(lambda t, ssem, zz, ss, own: piece(sec, i, t, ssem, zz, ss, own), i, t, own, act)
        act(piece(sec, i, t, send_x.at[t, i], z, xnb, own))
        act(piece(sec, i, t, send_y.at[t, i], z, ynb, own))
        act(piece(sec, i, t, send_sib.at[t, i], z, sib, own))

    def fan_right(t, own, act):
        along(lambda t, ssem, zz, ss, own: rpiece(core, t, ssem, zz, ss, own), 2, t, own, act)
        if not own:
            act(rpiece(core, t, send_sib.at[t, 8], z, sib))

    def fan_x(i, t, act):
        if i == 0:
            act(piece(xnb, i, t, send_y.at[t, 2], z, ynb))
        act(piece(xnb, i, t, send_sib.at[t, 2 + i], z, sib))

    def fan_y(i, t, act):
        if i == 1:
            act(piece(ynb, i, t, send_x.at[t, 2], z, xnb))
        act(piece(ynb, i, t, send_sib.at[t, 4 + i], z, sib))

    def fan_d(i, t, act):
        act(piece(dnb, i, t, send_sib.at[t, 6 + i], z, sib))

    start = lambda copy: copy.start()
    drain = lambda copy: copy.wait_send()

    t0 = order[0]
    for i in range(2):
        fan_own(i, t0, True, start)
    fan_right(t0, True, start)

    for s in range(sectors):
        value = jnp.int32(0)
        for p in range(1, sectors):
            value = jnp.where(lsec[p] == s, p, value)
        inverse[s] = value
        right_of[s] = rsec[value]

    row_at = lax.broadcasted_iota(jnp.int32, (width, width), 0)
    col_at = lax.broadcasted_iota(jnp.int32, (width, width), 1)

    own_w.wait()

    @pl.loop(0, sectors)
    def _(s):
        live = (row_at < lsize[s]) & (col_at < rsize[right_of[s]])
        high, low = split(jnp.where(live, wbuf[inverse[s]], 0.0))
        rows = pl.ds(pl.multiple_of(s * width, width), width)
        mcat[rows, :width] = high
        mcat[rows, width:] = low
        acc[s] = jnp.zeros((width, width), jnp.float32)

    own_r.wait()
    batch = 4 if sectors % 4 == 0 else 1

    def halfway(t):
        high, low = split(rbuf[t].reshape(rights * width, width))
        doubled = jnp.concatenate([high, high], axis=1)
        contract_last = (((1,), (1,)), ((), ()))

        @pl.loop(0, sectors // batch)
        def _(n):
            rows = pl.ds(pl.multiple_of(n * batch * width, batch * width), batch * width)
            left = mcat[rows, :]
            both = lax.dot_general(left, doubled, contract_last, preferred_element_type=jnp.float32)
            both += lax.dot_general(
                left[:, :width], low, contract_last, preferred_element_type=jnp.float32
            )
            for j in range(batch):
                s = n * batch + j
                mine = both[j * width : (j + 1) * width]
                which = jnp.full((width, width), right_of[s], jnp.int32)
                pick = mine[:, :width]
                for b in range(1, rights):
                    pick = jnp.where(which == b, mine[:, b * width : (b + 1) * width], pick)
                h_high, h_low = split(pick)
                hcat[t, s, :, :width] = h_high
                hcat[t, s, :, width:] = h_low

    def apply_left(s, t):
        high, low = split(lbuf[s, t])
        wide = jnp.dot(
            jnp.concatenate([high, low], axis=0), hcat[t, s], preferred_element_type=jnp.float32
        )
        acc[s] += wide[:width, :width] + (wide[:width, width:] + wide[width:, :width])

    def apply_group(group, t, wait):
        if wait:
            for i in range(2):
                await_l(group, i, t)
        for i in range(2):
            apply_left(2 * group + i, t)

    def land_own(k, i):
        await_l(sec, i, order[k])
        fan_own(i, order[k], False, start)

    def land_side(k, i):
        await_l(xnb, i, order[k])
        fan_x(i, order[k], start)
        await_l(ynb, i, order[k])
        fan_y(i, order[k], start)

    def land_far(k):
        for i in range(2):
            await_l(dnb, i, order[k])
            fan_d(i, order[k], start)

    def land_right(k):
        await_r(core, order[k])
        fan_right(order[k], False, start)

    def apply_side(k):
        apply_group(xnb, order[k], False)
        apply_group(ynb, order[k], False)
        apply_group(flip(xnb), order[k], True)
        apply_group(flip(ynb), order[k], True)

    def apply_far(k):
        apply_group(dnb, order[k], False)
        apply_group(flip(dnb), order[k], True)

    def apply_own(k):
        await_r(1 - core, order[k])
        halfway(order[k])
        apply_group(sec, order[k], False)
        apply_group(sib, order[k], True)

    middle = has_up & has_dn
    border = jnp.logical_not(middle)

    for copy in own_l:
        copy.wait()
    halfway(order[0])
    apply_group(sec, order[0], False)

    for i in range(2):
        land_own(1, i)
        land_side(0, i)

    @pl.when(middle)
    def _():
        for i in range(2):
            land_own(2, i)

    apply_group(sib, order[0], True)
    apply_side(0)
    land_right(1)
    land_side(1, 0)
    apply_own(1)
    land_side(1, 1)

    @pl.when(border)
    def _():
        for i in range(2):
            land_own(2, i)

    @pl.when(middle)
    def _():
        for i in range(2):
            land_own(3, i)
        land_right(2)

    land_far(0)
    apply_side(1)

    @pl.when(border)
    def _():
        for i in range(2):
            land_own(3, i)

    @pl.when(middle)
    def _():
        land_right(3)

    for i in range(2):
        land_side(2, i)
    apply_far(0)

    @pl.when(border)
    def _():
        land_right(2)

    apply_own(2)
    for i in range(2):
        land_side(3, i)
    apply_side(2)

    @pl.when(border)
    def _():
        land_right(3)

    apply_own(3)
    land_far(1)
    apply_side(3)
    land_far(2)
    apply_far(1)
    land_far(3)
    apply_far(2)
    apply_far(3)

    @pl.loop(0, sectors)
    def _(p):
        s = lsec[p]
        live = (row_at < lsize[s]) & (col_at < rsize[rsec[p]])
        out_ref[p] = jnp.where(live, acc[s], 0.0)

    for k in range(terms):
        t = order[k]
        for i in range(2):
            fan_own(i, t, k == 0, drain)
            fan_x(i, t, drain)
            fan_y(i, t, drain)
            fan_d(i, t, drain)
        fan_right(t, k == 0, drain)


def local_shards(wavefunction, left_sector, right_sector, left_size, right_size, left_ops, right_ops):
    terms = lax.axis_size("ops")
    sectors, width = left_size.shape[0], wavefunction.shape[1]
    rights = right_size.shape[0]
    dma = pltpu.SemaphoreType.DMA
    anywhere = pl.BlockSpec(memory_space=pl.ANY)
    scalars = pl.BlockSpec(memory_space=pltpu.SMEM)
    return pl.pallas_call(
        gather_contract,
        out_shape=jax.ShapeDtypeStruct(wavefunction.shape, jnp.float32),
        in_specs=[anywhere] * 3 + [scalars] * 4,
        out_specs=pl.BlockSpec(memory_space=pltpu.VMEM),
        scratch_shapes=[
            pltpu.VMEM((sectors, width, width), jnp.float32),
            pltpu.VMEM((sectors, terms, width, width), jnp.float32),
            pltpu.VMEM((terms, rights, width, width), jnp.float32),
            pltpu.VMEM((sectors * width, 2 * width), jnp.bfloat16),
            pltpu.VMEM((terms, sectors, width, 2 * width), jnp.bfloat16),
            pltpu.VMEM((sectors, width, width), jnp.float32),
            pltpu.SMEM((sectors,), jnp.int32),
            pltpu.SMEM((sectors,), jnp.int32),
            dma((2,)),
            dma((sectors, terms)),
            dma((terms, 2)),
            dma((terms, 3)),
            dma((terms, 3)),
            dma((terms, 3)),
            dma((terms, 3)),
            dma((terms, 9)),
        ],
        compiler_params=pltpu.CompilerParams(collective_id=0, has_side_effects=True),
    )(wavefunction, left_ops, right_ops, left_sector, right_sector, left_size, right_size)


def cube_shards(*arrays):
    wavefunction, left_size, left_ops = arrays[0], arrays[3], arrays[5]
    sectors, width = left_size.shape[0], wavefunction.shape[1]
    terms = lax.axis_size("ops")
    every_sector = wavefunction.shape[0] == sectors
    cube = lax.axis_size("sec") == 2**3 and terms == 2**2 and left_ops.shape[:2] == (2, 1)
    small = sectors * terms * width * width * 4 <= 2**23
    if every_sector and cube and small:
        return local_shards(*arrays)
    return shards(*arrays)


def solution(mesh):
    placed = (
        P(("ops", "sec"), None, None),
        P(("ops", "sec")),
        P(("ops", "sec")),
        P(),
        P(),
        P("sec", "ops", None, None),
        P(None, "ops", None, None),
    )
    return jax.shard_map(
        cube_shards, mesh=mesh, in_specs=placed, out_specs=P(("ops", "sec"), None, None), check_vma=False
    )
```

```python
import jax
import jax.numpy as jnp
from jax import lax
from jax.experimental import pallas as pl
from jax.experimental.pallas import tpu as pltpu
from jax.sharding import PartitionSpec as P

MESH = pl.DeviceIdType.MESH


def contract(running, packed, left_ids, right_ids, live_count, left_blocks, right_blocks):
    turn_count = (live_count + 1) // 2

    def advance(turn_index, current):
        first = 2 * turn_index
        block = lax.dynamic_slice_in_dim(packed, first, 2, 0)
        left_sel = lax.dynamic_slice_in_dim(left_ids, first, 2, 0)
        right_sel = lax.dynamic_slice_in_dim(right_ids, first, 2, 0)
        left_pick = left_blocks[left_sel]
        right_pick = right_blocks[right_sel]
        halfway = jnp.einsum("sij,stlj->stil", block, right_pick, precision=lax.Precision.HIGHEST)
        update = jnp.einsum("stmi,stil->sml", left_pick, halfway, precision=lax.Precision.HIGHEST)
        before = lax.dynamic_slice_in_dim(current, first, 2, 0)
        return lax.dynamic_update_slice_in_dim(current, before + update, first, 0)

    return lax.fori_loop(0, turn_count, advance, running)


def gather_whole(left_ops, right_ops):
    return (
        lax.all_gather(left_ops, "ops", axis=1, tiled=True),
        lax.all_gather(right_ops, "ops", axis=1, tiled=True),
    )


def arrange(incoming, tags, slot_count, width):
    incoming = incoming.reshape(slot_count, width, width)
    tag_ids = tags.reshape(slot_count).astype(jnp.int32)
    live_flag = (tag_ids > 0).astype(jnp.int32)
    order = jnp.argsort(1 - live_flag, stable=True)
    live_count = jnp.sum(live_flag)
    packed = incoming[order]
    right_ids = jnp.maximum(tag_ids[order] - 1, 0)
    return (packed, right_ids, order, live_count)


def shards(wavefunction, left_sector, right_sector, left_size, right_size, left_ops, right_ops):
    peer_count = lax.axis_size("sec")
    sec_local = left_ops.shape[0]
    width = wavefunction.shape[1]
    position = jnp.arange(width)
    left_live = jnp.sum(
        jnp.where(
            left_sector[:, None] == jnp.arange(left_size.shape[0])[None, :], left_size[None, :], 0
        ),
        axis=1,
    )
    right_live = jnp.sum(
        jnp.where(
            right_sector[:, None] == jnp.arange(right_size.shape[0])[None, :],
            right_size[None, :],
            0,
        ),
        axis=1,
    )
    row_live = position[None, :] < left_live[:, None]
    col_live = position[None, :] < right_live[:, None]
    window = (row_live[:, :, None] & col_live[:, None, :]).astype(jnp.float32)
    masked = wavefunction * window
    owner = left_sector // sec_local
    within = left_sector % sec_local
    outgoing = (
        jnp.zeros((peer_count, sec_local, width, width), jnp.float32).at[owner, within].set(masked)
    )
    labels = (
        jnp.zeros((peer_count, sec_local), jnp.float32)
        .at[owner, within]
        .set((right_sector + 1).astype(jnp.float32))
    )
    incoming, tags = (
        lax.all_to_all(outgoing, "sec", split_axis=0, concat_axis=0, tiled=True),
        lax.all_to_all(labels, "sec", split_axis=0, concat_axis=0, tiled=True),
    )
    slot_count = peer_count * sec_local
    packed, right_ids, order, live_count = arrange(incoming, tags, slot_count, width)
    left_ids = order % sec_local
    empty = jnp.zeros_like(packed)
    left_all, right_all = gather_whole(left_ops, right_ops)
    result = contract(empty, packed, left_ids, right_ids, live_count, left_all, right_all)
    restored = jnp.zeros_like(result).at[order].set(result)
    returned = lax.all_to_all(
        restored.reshape(peer_count, sec_local, width, width),
        "sec",
        split_axis=0,
        concat_axis=0,
        tiled=True,
    )
    return returned[owner, within] * window


def term_orders(count):
    orders = []
    for here in range(count):
        orders.append(sorted(range(count), key=lambda t: (abs(t - here), abs(2 * t - count + 1), t)))
    return orders


def split(value):
    high = value.astype(jnp.bfloat16)
    low = (value - high.astype(jnp.float32)).astype(jnp.bfloat16)
    return high, low


def gather_contract(
    wf_hbm, lops_hbm, rops_hbm, lsec, rsec, lsize, rsize,
    out,
    out_ref, out_sem, wbuf, lbuf, rbuf, mcat, hcat, acc, inverse, right_of,
    own_sem, recv_l, recv_r, send_x, send_y, send_up, send_dn, send_sib,
):
    terms = lax.axis_size("ops")
    sectors, _, width, _ = lbuf.shape
    rights = rbuf.shape[1]
    half = width // 2
    z = lax.axis_index("ops")
    sec = lax.axis_index("sec")
    core = sec % 2
    xpos = (sec // 2) % 2
    ypos = sec // 4
    sib = sec + 1 - 2 * core
    xnb = sec + 2 - 4 * xpos
    ynb = sec + 4 - 8 * ypos
    dnb = xnb + 4 - 8 * ypos
    has_up = z < terms - 1
    has_dn = z > 0
    table = term_orders(terms)
    order = []
    for k in range(terms):
        value = table[0][k] * 1
        for here in range(1, terms):
            value = jnp.where(z == here, table[here][k], value)
        order.append(value)

    def flip(group):
        return group + 1 - 2 * core

    barrier = pltpu.get_barrier_semaphore()

    def greet(zz, ss):
        pl.semaphore_signal(barrier, inc=1, device_id=(zz, ss), device_id_type=MESH)

    for peer in (sib, xnb, ynb):
        greet(z, peer)

    @pl.when(has_up)
    def _():
        greet(z + 1, sec)

    @pl.when(has_dn)
    def _():
        greet(z - 1, sec)

    own_l = [
        pltpu.make_async_copy(lops_hbm.at[i, 0], lbuf.at[2 * sec + i, z], recv_l.at[2 * sec + i, z])
        for i in range(2)
    ]
    own_r = pltpu.make_async_copy(rops_hbm.at[:, 0], rbuf.at[z], own_sem.at[0])
    own_w = pltpu.make_async_copy(wf_hbm, wbuf, own_sem.at[1])
    own_w.start()
    own_r.start()
    for copy in own_l:
        copy.start()
    pl.semaphore_wait(barrier, 3 + has_up.astype(jnp.int32) + has_dn.astype(jnp.int32))

    def move(src, dst, ssem, rsem, zz, ss):
        return pltpu.make_async_remote_copy(
            src_ref=src, dst_ref=dst, send_sem=ssem, recv_sem=rsem,
            device_id=(zz, ss), device_id_type=MESH,
        )

    def piece(group, i, t, ssem, zz, ss, own=False):
        s = 2 * group + i
        src = lops_hbm.at[i, 0] if own else lbuf.at[s, t]
        return move(src, lbuf.at[s, t], ssem, recv_l.at[s, t], zz, ss)

    def rpiece(h, t, ssem, zz, ss, own=False):
        rows = pl.ds(pl.multiple_of(h * half, half), half)
        src = rops_hbm.at[:, 0, rows] if own else rbuf.at[t, :, rows]
        return move(src, rbuf.at[t, :, rows], ssem, recv_r.at[t, h], zz, ss)

    def await_l(group, i, t):
        piece(group, i, t, send_x.at[t, 0], z, xnb).wait_recv()

    def await_r(h, t):
        rpiece(h, t, send_x.at[t, 0], z, xnb).wait_recv()

    def along(make, j, t, own, act):
        up = has_up & (t <= z)
        dn = has_dn & (t >= z)

        @pl.when(up)
        def _():
            act(make(t, send_up.at[t, j], z + 1, sec, own))

        @pl.when(dn)
        def _():
            act(make(t, send_dn.at[t, j], z - 1, sec, own))

    def fan_own(i, t, own, act):
        along(lambda t, ssem, zz, ss, own: piece(sec, i, t, ssem, zz, ss, own), i, t, own, act)
        act(piece(sec, i, t, send_x.at[t, i], z, xnb, own))
        act(piece(sec, i, t, send_y.at[t, i], z, ynb, own))
        act(piece(sec, i, t, send_sib.at[t, i], z, sib, own))

    def fan_right(t, own, act):
        along(lambda t, ssem, zz, ss, own: rpiece(core, t, ssem, zz, ss, own), 2, t, own, act)
        if not own:
            act(rpiece(core, t, send_sib.at[t, 8], z, sib))

    def fan_x(i, t, act):
        if i == 0:
            act(piece(xnb, i, t, send_y.at[t, 2], z, ynb))
        act(piece(xnb, i, t, send_sib.at[t, 2 + i], z, sib))

    def fan_y(i, t, act):
        if i == 1:
            act(piece(ynb, i, t, send_x.at[t, 2], z, xnb))
        act(piece(ynb, i, t, send_sib.at[t, 4 + i], z, sib))

    def fan_d(i, t, act):
        act(piece(dnb, i, t, send_sib.at[t, 6 + i], z, sib))

    start = lambda copy: copy.start()
    drain = lambda copy: copy.wait_send()

    t0 = order[0]
    for i in range(2):
        fan_own(i, t0, True, start)
    fan_right(t0, True, start)

    for s in range(sectors):
        value = jnp.int32(0)
        for p in range(1, sectors):
            value = jnp.where(lsec[p] == s, p, value)
        inverse[s] = value
        right_of[s] = rsec[value]

    row_at = lax.broadcasted_iota(jnp.int32, (width, width), 0)
    col_at = lax.broadcasted_iota(jnp.int32, (width, width), 1)

    own_w.wait()

    @pl.loop(0, sectors)
    def _(s):
        live = (row_at < lsize[s]) & (col_at < rsize[right_of[s]])
        high, low = split(jnp.where(live, wbuf[inverse[s]], 0.0))
        rows = pl.ds(pl.multiple_of(s * width, width), width)
        mcat[rows, :width] = high
        mcat[rows, width:] = low
        acc[s] = jnp.zeros((width, width), jnp.float32)

    own_r.wait()
    batch = 4 if sectors % 4 == 0 else 1

    def halfway(t):
        high, low = split(rbuf[t].reshape(rights * width, width))
        doubled = jnp.concatenate([high, high], axis=1)
        contract_last = (((1,), (1,)), ((), ()))

        @pl.loop(0, sectors // batch)
        def _(n):
            rows = pl.ds(pl.multiple_of(n * batch * width, batch * width), batch * width)
            left = mcat[rows, :]
            both = lax.dot_general(left, doubled, contract_last, preferred_element_type=jnp.float32)
            both += lax.dot_general(
                left[:, :width], low, contract_last, preferred_element_type=jnp.float32
            )
            for j in range(batch):
                s = n * batch + j
                mine = both[j * width : (j + 1) * width]
                which = jnp.full((width, width), right_of[s], jnp.int32)
                pick = mine[:, :width]
                for b in range(1, rights):
                    pick = jnp.where(which == b, mine[:, b * width : (b + 1) * width], pick)
                h_high, h_low = split(pick)
                hcat[t, s, :, :width] = h_high
                hcat[t, s, :, width:] = h_low

    def apply_left(s, t):
        high, low = split(lbuf[s, t])
        wide = jnp.dot(
            jnp.concatenate([high, low], axis=0), hcat[t, s], preferred_element_type=jnp.float32
        )
        acc[s] += wide[:width, :width] + (wide[:width, width:] + wide[width:, :width])

    def apply_group(group, t, wait):
        if wait:
            for i in range(2):
                await_l(group, i, t)
        for i in range(2):
            apply_left(2 * group + i, t)

    def land_own(k, i):
        await_l(sec, i, order[k])
        fan_own(i, order[k], False, start)

    def land_side(k, i):
        await_l(xnb, i, order[k])
        fan_x(i, order[k], start)
        await_l(ynb, i, order[k])
        fan_y(i, order[k], start)

    def land_far(k):
        for i in range(2):
            await_l(dnb, i, order[k])
            fan_d(i, order[k], start)

    def land_right(k):
        await_r(core, order[k])
        fan_right(order[k], False, start)

    def apply_side(k):
        apply_group(xnb, order[k], False)
        apply_group(ynb, order[k], False)
        apply_group(flip(xnb), order[k], True)
        apply_group(flip(ynb), order[k], True)

    def apply_far(k):
        apply_group(dnb, order[k], False)
        apply_group(flip(dnb), order[k], True)

    def apply_own(k):
        await_r(1 - core, order[k])
        halfway(order[k])
        apply_group(sec, order[k], False)
        apply_group(sib, order[k], True)

    middle = has_up & has_dn
    border = jnp.logical_not(middle)

    for copy in own_l:
        copy.wait()
    halfway(order[0])
    apply_group(sec, order[0], False)

    for i in range(2):
        land_own(1, i)
        land_side(0, i)

    @pl.when(middle)
    def _():
        for i in range(2):
            land_own(2, i)

    apply_group(sib, order[0], True)
    apply_side(0)
    land_right(1)
    land_side(1, 0)
    apply_own(1)
    land_side(1, 1)

    @pl.when(border)
    def _():
        for i in range(2):
            land_own(2, i)

    @pl.when(middle)
    def _():
        for i in range(2):
            land_own(3, i)
        land_right(2)

    land_far(0)
    apply_side(1)

    @pl.when(border)
    def _():
        for i in range(2):
            land_own(3, i)

    @pl.when(middle)
    def _():
        land_right(3)

    for i in range(2):
        land_side(2, i)
    apply_far(0)

    @pl.when(border)
    def _():
        land_right(2)

    apply_own(2)
    for i in range(2):
        land_side(3, i)
    apply_side(2)

    @pl.when(border)
    def _():
        land_right(3)

    land_far(1)
    apply_own(3)
    apply_far(1)
    land_far(2)
    apply_side(3)
    land_far(3)
    apply_far(2)
    apply_far(3)

    for p in range(sectors):
        s = lsec[p]
        live = (row_at < lsize[s]) & (col_at < rsize[rsec[p]])
        out_ref[p] = jnp.where(live, acc[s], 0.0)
        pltpu.make_async_copy(out_ref.at[p], out.at[p], out_sem.at[p]).start()

    for k in range(terms):
        t = order[k]
        for i in range(2):
            fan_own(i, t, k == 0, drain)
            fan_x(i, t, drain)
            fan_y(i, t, drain)
            fan_d(i, t, drain)
        fan_right(t, k == 0, drain)

    for p in range(sectors):
        pltpu.make_async_copy(out_ref.at[p], out.at[p], out_sem.at[p]).wait()


def local_shards(wavefunction, left_sector, right_sector, left_size, right_size, left_ops, right_ops):
    terms = lax.axis_size("ops")
    sectors, width = left_size.shape[0], wavefunction.shape[1]
    rights = right_size.shape[0]
    dma = pltpu.SemaphoreType.DMA
    anywhere = pl.BlockSpec(memory_space=pl.ANY)
    scalars = pl.BlockSpec(memory_space=pltpu.SMEM)
    return pl.pallas_call(
        gather_contract,
        out_shape=jax.ShapeDtypeStruct(wavefunction.shape, jnp.float32),
        in_specs=[anywhere] * 3 + [scalars] * 4,
        out_specs=anywhere,
        scratch_shapes=[
            pltpu.VMEM(wavefunction.shape, jnp.float32),
            dma((sectors,)),
            pltpu.VMEM((sectors, width, width), jnp.float32),
            pltpu.VMEM((sectors, terms, width, width), jnp.float32),
            pltpu.VMEM((terms, rights, width, width), jnp.float32),
            pltpu.VMEM((sectors * width, 2 * width), jnp.bfloat16),
            pltpu.VMEM((terms, sectors, width, 2 * width), jnp.bfloat16),
            pltpu.VMEM((sectors, width, width), jnp.float32),
            pltpu.SMEM((sectors,), jnp.int32),
            pltpu.SMEM((sectors,), jnp.int32),
            dma((2,)),
            dma((sectors, terms)),
            dma((terms, 2)),
            dma((terms, 3)),
            dma((terms, 3)),
            dma((terms, 3)),
            dma((terms, 3)),
            dma((terms, 9)),
        ],
        compiler_params=pltpu.CompilerParams(collective_id=0, has_side_effects=True),
    )(wavefunction, left_ops, right_ops, left_sector, right_sector, left_size, right_size)


def cube_shards(*arrays):
    wavefunction, left_size, left_ops = arrays[0], arrays[3], arrays[5]
    sectors, width = left_size.shape[0], wavefunction.shape[1]
    terms = lax.axis_size("ops")
    every_sector = wavefunction.shape[0] == sectors
    cube = lax.axis_size("sec") == 2**3 and terms == 2**2 and left_ops.shape[:2] == (2, 1)
    small = sectors * terms * width * width * 4 <= 2**23
    if every_sector and cube and small:
        return local_shards(*arrays)
    return shards(*arrays)


def solution(mesh):
    placed = (
        P(("ops", "sec"), None, None),
        P(("ops", "sec")),
        P(("ops", "sec")),
        P(),
        P(),
        P("sec", "ops", None, None),
        P(None, "ops", None, None),
    )
    return jax.shard_map(
        cube_shards, mesh=mesh, in_specs=placed, out_specs=P(("ops", "sec"), None, None), check_vma=False
    )
```
